32 devices in a mesh: groups: 2 (over x), tiles: 16 (over z, y, core).
Axes of the slice: x: 2, y: 2, z: 4, core: 2. Of those that a mesh axis runs over, the one named last changes fastest.
Arguments:
- pieces: bfloat16 [512, 6, 128, 128], P(('groups', 'tiles')), parts along dimension 0, may hold values from -6 to 6
- piece_blend: int32 [512], P(('groups', 'tiles')), parts along dimension 0, may hold values from 0 to 63, as said below
- corners: int32 [512, 2], P(('groups', 'tiles')), parts along dimension 0, may hold values from -96 to 223
- blend_home: int32 [128], P('groups'), parts along dimension 0, may hold values from 0 to 63, as said below
- source_count: int32 [128], P(('groups', 'tiles')), parts along dimension 0, may hold values from 1 to 4
- footprint: int32 [128, 128, 128], P(('groups', 'tiles')), parts along dimension 0, may hold values from 0 to 4
- spectra: float32 [128, 4, 6], P(('groups', 'tiles')), parts along dimension 0, may hold values from 0.2 to 1
- giant_pieces: bfloat16 [32, 6, 128, 128], P(('groups', 'tiles')), parts along dimension 0, may hold values from -6 to 6
- giant_footprint: int32 [32, 128, 128], P(('groups', 'tiles')), parts along dimension 0, may hold values from 0 to 4
- giant_spectra: float32 [32, 4, 6], P(('groups', 'tiles')), parts along dimension 0, may hold values from 0.2 to 1
- psf_matrix: bfloat16 [6, 128, 128], replicated, may hold values from 0 to 1
Outputs:
- blend_morph: bfloat16 [128, 4, 128, 128], P(('groups', 'tiles')), parts along dimension 0
- blend_spectra: bfloat16 [128, 4, 6], P(('groups', 'tiles')), parts along dimension 0
- tile_model: float32 [32, 6, 256, 256], P(('groups', 'tiles')), parts along dimension 0
- giant_morph: float32 [32, 4, 128, 128], P(('groups', 'tiles')), parts along dimension 0
The draws below stay inside these ranges and needn't reach their ends.
There are 2 independent parts, one for each index of `groups`. The reference program is written for one: setup_inputs(seed, part) draws one part's arguments, and reference() takes and returns one part's arrays. A program takes and returns all parts, laid end to end along the dimension named above; an argument that names none is the same for every part. Nothing has to cross between parts.
Inputs may be any that keep to these rules, and one draw needn't show every extreme that they name: `piece_blend`: at most 2 pieces of one device belong to blends of one owner; in every draw some owner gets exactly 2 pieces from every device. `blend_home`: A permutation of 0 to 63.
All inputs are finite; a program needn't handle non-finite values.
Results may differ from the reference program's by a relative error of at most 0.006.
Values may be sent and summed in bfloat16 or wider, within the bound.
A program may use at most 128 MiB of HBM per device.

```python
import math
import jax
import jax.numpy as jnp
from jax import lax

BANDS = 6
PIX = 128
SRC = 4
GSRC = 4
SLOT_CAP = 2
TILE = 256
ITERS = 3
PIECE_DEV = 16
BLEND_DEV = 4
PIECES = 256
BLENDS = 64
N_TILES = 16


def route_table(key):
    base_key = jax.random.fold_in(key, 7)
    key_hot, key_pref, key_score, key_slot, key_perm, key_order = jax.random.split(base_key, 6)
    slot_load_total = N_TILES * SLOT_CAP
    busiest_owner = jax.random.randint(key_hot, (), 0, N_TILES)
    owner_preference = jax.random.randint(key_pref, (N_TILES,), 0, 4000)
    placement_scores = jax.random.randint(key_score, (N_TILES, slot_load_total), 0, 4000)
    destination_for = jnp.arange(slot_load_total, dtype=jnp.int32) // SLOT_CAP
    extra_reward = owner_preference[destination_for] + jnp.where(destination_for == busiest_owner, 100000, 0)
    running_totals = (placement_scores + extra_reward[None, :]) * slot_load_total + jnp.arange(slot_load_total, dtype=jnp.int32)[None, :]
    unused, chosen = lax.top_k(running_totals, PIECE_DEV)
    dests = chosen // SLOT_CAP
    order_keys = jax.random.randint(key_order, (N_TILES, PIECE_DEV), 0, 1 << 20) * PIECE_DEV + jnp.arange(PIECE_DEV, dtype=jnp.int32)[None, :]
    order = jnp.argsort(order_keys, axis=1)
    dests = jnp.take_along_axis(dests, order, axis=1)
    places = jax.random.randint(key_slot, (N_TILES, PIECE_DEV), 0, BLEND_DEV)
    homes = (dests * BLEND_DEV + places).reshape(-1)
    blend_at_home = jax.random.permutation(key_perm, BLENDS).astype(jnp.int32)
    piece_blend = blend_at_home[homes].astype(jnp.int32)
    blend_home = jnp.argsort(blend_at_home).astype(jnp.int32)
    return (piece_blend, blend_home)


def draw_piece_blend(key, part):
    return route_table(key)[0]


def draw_blend_home(key, part):
    return route_table(key)[1]


def group_labels(group_key):
    key_cells, key_row, key_col, key_label = jax.random.split(group_key, 4)
    cell_owner = (jax.random.permutation(key_cells, 32).astype(jnp.int32) % 8).astype(jnp.int32)
    row_shift = jax.random.randint(key_row, (), 0, PIX // 4) * 4 + 2
    col_shift = jax.random.randint(key_col, (), 0, PIX // 4) * 4 + 2
    rows = (jnp.arange(PIX, dtype=jnp.int32) + row_shift) % PIX
    cols = (jnp.arange(PIX, dtype=jnp.int32) + col_shift) % PIX
    cell = ((rows // (PIX // 4))[:, None] * 8 + (cols // (PIX // 8))[None, :]).astype(jnp.int32)
    pixel_owner = cell_owner[cell]
    labels = jax.random.randint(key_label, (8, PIX, PIX), 1, GSRC + 1)
    mine = pixel_owner[None, :, :] == jnp.arange(8, dtype=jnp.int32)[:, None, None]
    return jnp.where(mine, labels, 0).astype(jnp.int32)


def draw_giant_footprint(key, part):
    base_key = jax.random.fold_in(key, 11)
    group_keys = jax.random.split(base_key, N_TILES // 8)
    return jax.vmap(group_labels)(group_keys).reshape(N_TILES, PIX, PIX).astype(jnp.int32)


def draw_psf_matrix(key, part):
    row_ids = jnp.arange(PIX, dtype=jnp.float32)[:, None]
    col_ids = jnp.arange(PIX, dtype=jnp.float32)[None, :]
    offset = row_ids - col_ids
    band_ids = jnp.arange(BANDS, dtype=jnp.float32)[:, None, None]
    spread = 1.5 + 0.5 * band_ids
    rough = jax.random.uniform(key, (BANDS, PIX, PIX), jnp.float32, 0.5, 1.5)
    weights = jnp.exp(-offset[None] ** 2 / (2.0 * spread ** 2)) * rough * (jnp.abs(offset)[None] <= 12.0)
    return (weights / jnp.sum(weights, axis=2, keepdims=True)).astype(jnp.bfloat16)


def with_ends(array, stream_key, least, high):
    spot = [jax.random.randint(jax.random.fold_in(stream_key, axis), (), 0, length) for axis, length in enumerate(array.shape)]
    widest = array.shape.index(max(array.shape))
    next_to = spot[:widest] + [(spot[widest] + 1) % array.shape[widest]] + spot[widest + 1:]
    return array.at[tuple(spot)].set(least).at[tuple(next_to)].set(high)


def steps_of(rng, extent, shards, smallest, top_value):
    gain = 1.0
    for position, blocks in shards:
        heights = jax.random.uniform(jax.random.fold_in(jax.random.fold_in(rng, 6), position), (blocks,), jnp.float32, smallest / len(shards), top_value / len(shards))
        gain = gain * jnp.repeat(jnp.exp(heights), extent[position] // blocks).reshape((-1,) + (1,) * (len(extent) - 1 - position))
    return gain


def noise(key, extent, width, most, cuts=(), held_as=jnp.bfloat16):
    array = jax.random.normal(key, extent, jnp.float32) * width
    if len(cuts) > 0:
        array = steps_of(key, extent, cuts, -0.22, 0.18) * array
    return jnp.clip(array, min=-most, max=most).astype(held_as)


def setup_inputs(seed: int = 0, part: int = 0) -> dict:
    key_list = jax.random.split(jax.random.key(seed), 12)
    part_keys = jax.random.split(jax.random.fold_in(key_list[11], part), 12)
    return {
        "pieces": noise(part_keys[0], (PIECES, BANDS, PIX, PIX), 1.0, 6.0, ((0, 16),)),
        "piece_blend": draw_piece_blend(jax.random.fold_in(jax.random.fold_in(key_list[11], part), 71), part),
        "corners": with_ends(jax.random.randint(part_keys[2], (PIECES, 2), 0 - (PIX - PIX // 4), TILE - PIX // 4), jax.random.fold_in(part_keys[2], 1), 0 - (PIX - PIX // 4), (TILE - PIX // 4) - 1).astype(jnp.int32),
        "blend_home": draw_blend_home(jax.random.fold_in(jax.random.fold_in(key_list[11], part), 71), part),
        "source_count": with_ends(jax.random.randint(part_keys[4], (BLENDS,), 1, SRC + 1), jax.random.fold_in(part_keys[4], 1), 1, SRC).astype(jnp.int32),
        "footprint": with_ends(jax.random.randint(part_keys[5], (BLENDS, PIX, PIX), 0, SRC + 1), jax.random.fold_in(part_keys[5], 1), 0, SRC).astype(jnp.int32),
        "spectra": jnp.clip(jnp.exp(math.log(1.0) - 1.609438 * jax.random.uniform(part_keys[6], (BLENDS, SRC, BANDS), jnp.float32) ** steps_of(part_keys[6], (BLENDS, SRC, BANDS), ((0, 16),), -0.2, 0.2)), 0.2, 1.0),
        "giant_pieces": noise(part_keys[7], (N_TILES, BANDS, PIX, PIX), 1.0, 6.0, ((0, 16),)),
        "giant_footprint": draw_giant_footprint(jax.random.fold_in(jax.random.fold_in(key_list[11], part), 71), part),
        "giant_spectra": jnp.clip(jnp.exp(math.log(1.0) - 1.609438 * jax.random.uniform(part_keys[9], (N_TILES, GSRC, BANDS), jnp.float32) ** steps_of(part_keys[9], (N_TILES, GSRC, BANDS), ((0, 16),), -0.2, 0.2)), 0.2, 1.0),
        "psf_matrix": draw_psf_matrix(jax.random.fold_in(key_list[11], 71), part),
    }


step_size = 0.1


def psf_blur(mix, psf_matrix):
    kernel = psf_matrix.astype(jnp.float32)
    half_way = jnp.einsum('bij,nbjk->nbik', kernel, mix.astype(jnp.float32)).astype(jnp.bfloat16)
    return jnp.einsum('nbij,bkj->nbik', half_way.astype(jnp.float32), kernel)


def adjoint(resid, psf_matrix):
    kernel = psf_matrix.astype(jnp.float32)
    half_way = jnp.einsum('bji,nbjk->nbik', kernel, resid.astype(jnp.float32)).astype(jnp.bfloat16)
    return jnp.einsum('nbij,bjk->nbik', half_way.astype(jnp.float32), kernel)


def combine(sed, morph):
    return jnp.einsum('nkb,nkij->nbij', sed, morph, precision=lax.Precision.HIGHEST)


def initial(image, labels, active):
    source_total = active.shape[1]
    base_map = jnp.maximum(jnp.mean(image, axis=1), 0.0)
    marks = (labels[:, None] == (jnp.arange(source_total, dtype=jnp.int32) + 1)[None, :, None, None]).astype(jnp.float32)
    return marks * base_map[:, None] * active[:, :, None, None]


def refine(image, morph, sed, active, psf_matrix, total):
    for iteration in range(ITERS):
        model_now = total(psf_blur(combine(sed, morph).astype(jnp.bfloat16), psf_matrix))
        resid = (image - model_now).astype(jnp.bfloat16)
        grad = adjoint(resid, psf_matrix)
        inner = jnp.einsum('nkij,nbij->nkb', morph, grad, precision=lax.Precision.HIGHEST)
        energy = jnp.sum(morph * morph, axis=(2, 3))
        push = jnp.einsum('nkb,nbij->nkij', sed, grad, precision=lax.Precision.HIGHEST)
        sed_next = jnp.maximum(sed + inner / (energy + 1.0)[:, :, None], 0.0) * active[:, :, None]
        morph = jnp.maximum(morph + step_size * push, 0.0) * active[:, :, None, None]
        sed = sed_next
    return morph, sed


def reference(pieces, piece_blend, corners, blend_home, source_count, footprint, spectra, giant_pieces, giant_footprint, giant_spectra, psf_matrix):
    piece_home = blend_home[piece_blend].astype(jnp.int32)
    flat = pieces.astype(jnp.float32).reshape(PIECES, BANDS * PIX * PIX)
    blend_image = jax.ops.segment_sum(flat, piece_home, num_segments=BLENDS).reshape(BLENDS, BANDS, PIX, PIX)
    active = (jnp.arange(SRC, dtype=jnp.int32)[None, :] < source_count[:, None]).astype(jnp.float32)

    def per_owner(owner_block):
        image, labels, start_sed, act = owner_block
        morph = initial(image, labels, act)
        sed = start_sed * act[:, :, None]
        morph, sed = refine(image, morph, sed, act, psf_matrix, lambda summed: summed)
        final_morph = morph.astype(jnp.bfloat16)
        final_sed = sed.astype(jnp.bfloat16)
        mix = combine(final_sed.astype(jnp.float32), final_morph.astype(jnp.float32)).astype(jnp.bfloat16)
        model = psf_blur(mix, psf_matrix).astype(jnp.bfloat16)
        return final_morph, final_sed, model

    blocks = (blend_image.reshape(N_TILES, BLEND_DEV, BANDS, PIX, PIX),
              footprint.reshape(N_TILES, BLEND_DEV, PIX, PIX),
              spectra.reshape(N_TILES, BLEND_DEV, SRC, BANDS),
              active.reshape(N_TILES, BLEND_DEV, SRC))
    final_morph, final_sed, models = lax.map(per_owner, blocks)
    final_morph = final_morph.reshape(BLENDS, SRC, PIX, PIX)
    final_sed = final_sed.reshape(BLENDS, SRC, BANDS)
    models = models.reshape(BLENDS, BANDS, PIX, PIX)

    margin = PIX - PIX // 4

    def per_tile(tile_block):
        spots, homes = tile_block
        canvas = jnp.zeros((BANDS, TILE + 2 * margin, TILE + 2 * margin), jnp.float32)

        def place(piece_index, canvas):
            patch_model = lax.dynamic_index_in_dim(models, homes[piece_index], 0, keepdims=False).astype(jnp.float32)
            row_start = (spots[piece_index, 0] + margin).astype(jnp.int32)
            col_start = (spots[piece_index, 1] + margin).astype(jnp.int32)
            anchor = (jnp.zeros((), jnp.int32), row_start, col_start)
            region = lax.dynamic_slice(canvas, anchor, (BANDS, PIX, PIX))
            return lax.dynamic_update_slice(canvas, region + patch_model, anchor)

        canvas = lax.fori_loop(0, PIECE_DEV, place, canvas)
        return canvas[:, margin:margin + TILE, margin:margin + TILE]

    tile_model = lax.map(per_tile, (corners.reshape(N_TILES, PIECE_DEV, 2), piece_home.reshape(N_TILES, PIECE_DEV)))

    group_count = N_TILES // 8

    def group_sum(field_sum):
        summed = field_sum.reshape((group_count, 8) + field_sum.shape[1:]).sum(axis=1)
        return jnp.repeat(summed, 8, axis=0)

    giant_image = group_sum(giant_pieces.astype(jnp.float32))
    giant_active = jnp.ones((N_TILES, GSRC), jnp.float32)
    giant_start = initial(giant_image, giant_footprint, giant_active)
    giant_morph, giant_sed = refine(giant_image, giant_start, giant_spectra, giant_active, psf_matrix, group_sum)
    return final_morph, final_sed, tile_model, giant_morph
```

```python
import functools

import jax
import jax.numpy as jnp
from jax import lax
from jax.experimental import pallas as pl
from jax.experimental.pallas import tpu as pltpu
from jax.sharding import PartitionSpec as P

TILE = 256
ITERS = 3
GROUP = 8
MESH = pl.DeviceIdType.MESH
F32 = jnp.float32
BF16 = jnp.bfloat16

step_size = 0.1

VMEM = pl.BlockSpec(memory_space=pltpu.VMEM)
SMEM = pl.BlockSpec(memory_space=pltpu.SMEM)
ANY = pl.BlockSpec(memory_space=pl.ANY)


def matmul(a, b):
    return jnp.dot(a, b, preferred_element_type=F32)


def matmul_t(a, b):
    return lax.dot_general(a, b, (((1,), (1,)), ((), ())), preferred_element_type=F32)


def t_matmul(a, b):
    return lax.dot_general(a, b, (((0,), (0,)), ((), ())), preferred_element_type=F32)


def barrier_all(me, count):
    barrier = pltpu.get_barrier_semaphore()
    for k in range(1, count):
        pl.semaphore_signal(
            barrier, inc=1, device_id={"tiles": lax.rem(me + k, count)}, device_id_type=MESH
        )
    pl.semaphore_wait(barrier, count - 1)


def remote(src, dst, send_sem, recv_sem, peer):
    return pltpu.make_async_remote_copy(
        src_ref=src,
        dst_ref=dst,
        send_sem=send_sem,
        recv_sem=recv_sem,
        device_id={"tiles": peer},
        device_id_type=MESH,
    )


def mix_band(sed_ref, morph_ref, b, bands, sources):
    total = sed_ref[b : b + 1, :] * morph_ref[0]
    for k in range(1, sources):
        row = k * bands + b
        total = total + sed_ref[row : row + 1, :] * morph_ref[k]
    return total.astype(BF16)


def blur_band(mix, kernel):
    return matmul_t(matmul(kernel, mix).astype(BF16), kernel)


def adjoint_band(resid, kernel):
    return matmul(t_matmul(kernel, resid).astype(BF16), kernel)


def update(sed_ref, morph_ref, grad_ref, part_ref, energy_ref, act_rows, bands, sources):
    for k in range(sources):
        morph = morph_ref[k]
        energy = jnp.sum(morph * morph, axis=0, keepdims=True)
        push = None
        for b in range(bands):
            row = k * bands + b
            grad = grad_ref[b]
            part_ref[row : row + 1, :] = jnp.sum(morph * grad, axis=0, keepdims=True)
            energy_ref[row : row + 1, :] = energy
            term = sed_ref[row : row + 1, :] * grad
            push = term if push is None else push + term
        fresh = jnp.maximum(morph + step_size * push, 0.0)
        if act_rows is not None:
            fresh = fresh * act_rows[k * bands : k * bands + 1, :]
        morph_ref[k] = fresh
    inner = jnp.sum(part_ref[...], axis=1, keepdims=True)
    energy = jnp.sum(energy_ref[...], axis=1, keepdims=True)
    sed = jnp.maximum(sed_ref[...] + inner / (energy + 1.0), 0.0)
    if act_rows is not None:
        sed = sed * act_rows[...]
    sed_ref[...] = sed


def first_kernel(
    count,
    bands,
    sources,
    pieces_ref,
    giant_ref,
    labels_ref,
    spectra_ref,
    psf_ref,
    recv_ref,
    morph_ref,
    scatter_buf,
    base_buf,
    resid_buf,
    blurred,
    image_part,
    sed_ref,
    grad_ref,
    part_ref,
    energy_ref,
    own_sem,
    send_sem,
    recv_sem,
    rs_send,
    rs_recv,
    ag_send,
    ag_recv,
):
    me = lax.axis_index("tiles")
    rank = lax.rem(me, GROUP)
    base = me - rank
    barrier_all(me, count)

    def scatter_copies(slot, src):
        copies = []
        for k in range(1, GROUP):
            other = lax.rem(rank + k, GROUP)
            copies.append(
                remote(
                    src.at[:, other],
                    scatter_buf.at[slot, rank],
                    rs_send.at[slot, k - 1],
                    rs_recv.at[slot, k - 1],
                    base + other,
                )
            )
        return copies

    def gather_copies(slot, ref):
        copies = []
        for k in range(1, GROUP):
            other = lax.rem(rank + k, GROUP)
            copies.append(
                remote(
                    ref.at[rank],
                    ref.at[rank],
                    ag_send.at[slot, k - 1],
                    ag_recv.at[slot, k - 1],
                    base + other,
                )
            )
        return copies

    def others_sum(slot, own):
        total = own.astype(F32)
        for k in range(1, GROUP):
            source = lax.rem(rank + GROUP - k, GROUP)
            total = total + scatter_buf[slot, source].astype(F32)
        return total

    opening = scatter_copies(ITERS, giant_ref)
    for copy in opening:
        copy.start()
    own = pltpu.make_async_copy(pieces_ref.at[:, me], recv_ref.at[me], own_sem)
    own.start()
    exchange = []
    for k in range(1, count):
        peer = lax.rem(me + k, count)
        copy = remote(
            pieces_ref.at[:, peer], recv_ref.at[me], send_sem.at[k - 1], recv_sem.at[k - 1], peer
        )
        copy.start()
        exchange.append(copy)

    for copy in opening:
        copy.wait_recv()
    image = others_sum(ITERS, giant_ref[:, rank])
    image_part[...] = image
    mean = image[0]
    for b in range(1, bands):
        mean = mean + image[b]
    base_buf[rank] = jnp.maximum(mean / bands, 0.0)
    spread = gather_copies(ITERS, base_buf)
    for copy in spread:
        copy.start()
    sed_ref[...] = spectra_ref[...]
    for copy in spread:
        copy.wait()
    for copy in opening:
        copy.wait_send()
    side = labels_ref.shape[0]
    base_map = base_buf[...].reshape(side, side)
    for k in range(sources):
        morph_ref[k] = jnp.where(labels_ref[...] == k + 1, base_map, 0.0)

    def iteration(it, carry):
        for b in range(bands):
            mix = mix_band(sed_ref, morph_ref, b, bands, sources)
            blurred[it, b] = (
                blur_band(mix, psf_ref[b]).astype(BF16).reshape(GROUP, side // GROUP, side)
            )
        sends = scatter_copies(it, blurred.at[it])
        for copy in sends:
            copy.start()
        for copy in sends:
            copy.wait()
        model = others_sum(it, blurred[it, :, rank])
        resid_buf[it, rank] = (image_part[...] - model).astype(BF16)
        shares = gather_copies(it, resid_buf.at[it])
        for copy in shares:
            copy.start()
        for copy in shares:
            copy.wait()
        for b in range(bands):
            resid = resid_buf[it, :, b].reshape(side, side)
            grad_ref[b] = adjoint_band(resid, psf_ref[b])
        update(sed_ref, morph_ref, grad_ref, part_ref, energy_ref, None, bands, sources)
        return carry

    lax.fori_loop(0, ITERS, iteration, 0)
    own.wait()
    for copy in exchange:
        copy.wait()


def segment_kernel(homes_ref, recv_ref, out_ref, total):
    total[...] = jnp.zeros_like(total)

    def add(index, carry):
        home = homes_ref[index]
        total[home] = total[home] + recv_ref[index].astype(F32)
        return carry

    lax.fori_loop(0, recv_ref.shape[0], add, 0, unroll=4)
    out_ref[...] = total[...].astype(BF16)


def owner_kernel(count, owned, src_ref, dst_ref, own_sem, send_sem, recv_sem):
    me = lax.axis_index("tiles")
    barrier_all(me, count)
    own = pltpu.make_async_copy(
        src_ref.at[pl.ds(me * owned, owned)], dst_ref.at[:, me], own_sem
    )
    own.start()
    copies = []
    for k in range(1, count):
        peer = lax.rem(me + k, count)
        copy = remote(
            src_ref.at[pl.ds(peer * owned, owned)],
            dst_ref.at[:, me],
            send_sem.at[k - 1],
            recv_sem.at[k - 1],
            peer,
        )
        copy.start()
        copies.append(copy)
    own.wait()
    for copy in copies:
        copy.wait()


def blend_kernel(
    bands,
    sources,
    image_ref,
    labels_ref,
    spectra_ref,
    active_ref,
    psf_ref,
    out_morph,
    out_sed,
    out_model,
    morph_ref,
    sed_ref,
    grad_ref,
    part_ref,
    energy_ref,
):
    act = active_ref.at[0]
    sed_ref[...] = spectra_ref[0] * active_ref[0]
    mean = image_ref[0, 0].astype(F32)
    for b in range(1, bands):
        mean = mean + image_ref[0, b].astype(F32)
    base_map = jnp.maximum(mean / bands, 0.0)
    for k in range(sources):
        morph_ref[k] = (
            jnp.where(labels_ref[0] == k + 1, base_map, 0.0) * act[k * bands : k * bands + 1, :]
        )

    def iteration(it, carry):
        for b in range(bands):
            kernel = psf_ref[b]
            mix = mix_band(sed_ref, morph_ref, b, bands, sources)
            resid = (image_ref[0, b].astype(F32) - blur_band(mix, kernel)).astype(BF16)
            grad_ref[b] = adjoint_band(resid, kernel)
        update(sed_ref, morph_ref, grad_ref, part_ref, energy_ref, act, bands, sources)
        return carry

    lax.fori_loop(0, ITERS, iteration, 0)
    out_morph[0] = morph_ref[...].astype(BF16)
    morph_ref[...] = morph_ref[...].astype(BF16).astype(F32)
    sed_ref[...] = sed_ref[...].astype(BF16).astype(F32)
    out_sed[0] = sed_ref[...]
    for b in range(bands):
        mix = mix_band(sed_ref, morph_ref, b, bands, sources)
        out_model[0, b] = blur_band(mix, psf_ref[b]).astype(BF16)


def return_kernel(
    count,
    owned,
    piece_count,
    homes_ref,
    model_ref,
    out_ref,
    held,
    picked,
    own_sems,
    send_sem,
    recv_sem,
    send_two,
    recv_two,
):
    me = lax.axis_index("tiles")
    barrier_all(me, count)
    own = pltpu.make_async_copy(
        model_ref.at[:, me], held.at[pl.ds(me * owned, owned)], own_sems.at[0]
    )
    own.start()
    copies = []
    for k in range(1, count):
        peer = lax.rem(me + k, count)
        copy = remote(
            model_ref.at[:, peer],
            held.at[pl.ds(me * owned, owned)],
            send_sem.at[k - 1],
            recv_sem.at[k - 1],
            peer,
        )
        copy.start()
        copies.append(copy)
    own.wait()
    for copy in copies:
        copy.wait()

    def pick(target):
        def one(index, carry):
            picked[target, index] = held[homes_ref[target * piece_count + index]]
            return carry

        lax.fori_loop(0, piece_count, one, 0)

    answers = []
    for k in range(1, count):
        peer = lax.rem(me + k, count)
        pick(peer)
        copy = remote(
            picked.at[peer], out_ref.at[:, me], send_two.at[k - 1], recv_two.at[k - 1], peer
        )
        copy.start()
        answers.append(copy)
    pick(me)
    last = pltpu.make_async_copy(picked.at[me], out_ref.at[:, me], own_sems.at[1])
    last.start()
    last.wait()
    for copy in answers:
        copy.wait()


def place_kernel(side, corners_ref, model_ref, out_ref, row_hot, col_hot):
    piece_count = model_ref.shape[0]

    @pl.when(pl.program_id(0) == 0)
    def _():
        rows = lax.broadcasted_iota(jnp.int32, (TILE, side), 0)
        inner = lax.broadcasted_iota(jnp.int32, (TILE, side), 1)
        inner_c = lax.broadcasted_iota(jnp.int32, (side, TILE), 0)
        cols = lax.broadcasted_iota(jnp.int32, (side, TILE), 1)

        def build(index, carry):
            row_hot[index] = jnp.where(rows == inner + corners_ref[index, 0], 1.0, 0.0).astype(BF16)
            col_hot[index] = jnp.where(cols == inner_c + corners_ref[index, 1], 1.0, 0.0).astype(
                BF16
            )
            return carry

        lax.fori_loop(0, piece_count, build, 0)

    total = jnp.zeros((TILE, TILE), F32)
    for index in range(piece_count):
        wide = matmul(model_ref[index, 0], col_hot[index]).astype(BF16)
        total = total + matmul(row_hot[index], wide)
    out_ref[0] = total


def on_device(
    pieces,
    piece_blend,
    corners,
    blend_home,
    source_count,
    footprint,
    spectra,
    giant_pieces,
    giant_footprint,
    giant_spectra,
    psf_matrix,
):
    count = lax.axis_size("tiles")
    piece_count, bands, side, _ = pieces.shape
    owned = footprint.shape[0]
    blend_count = blend_home.shape[0]
    sources = spectra.shape[1]
    rows = bands * side // count
    lanes = side
    table = sources * bands
    lookup = piece_blend[:, None] == jnp.arange(blend_count, dtype=jnp.int32)[None, :]
    piece_home = jnp.sum(jnp.where(lookup, blend_home[None, :], 0), axis=1)
    homes = lax.all_gather(piece_home, "tiles", axis=0, tiled=True)

    dma = pltpu.SemaphoreType.DMA
    strip = side // GROUP
    recv, giant_morph = pl.pallas_call(
        functools.partial(first_kernel, count, bands, sources),
        out_shape=(
            jax.ShapeDtypeStruct((count, piece_count, rows, lanes), BF16),
            jax.ShapeDtypeStruct((sources, side, side), F32),
        ),
        in_specs=[ANY, VMEM, VMEM, VMEM, VMEM],
        out_specs=(ANY, VMEM),
        scratch_shapes=[
            pltpu.VMEM((ITERS + 1, GROUP, bands, strip, side), BF16),
            pltpu.VMEM((GROUP, strip, side), F32),
            pltpu.VMEM((ITERS, GROUP, bands, strip, side), BF16),
            pltpu.VMEM((ITERS, bands, GROUP, strip, side), BF16),
            pltpu.VMEM((bands, strip, side), F32),
            pltpu.VMEM((table, lanes), F32),
            pltpu.VMEM((bands, side, side), F32),
            pltpu.VMEM((table, lanes), F32),
            pltpu.VMEM((table, lanes), F32),
            dma,
            dma((count - 1,)),
            dma((count - 1,)),
            dma((ITERS + 1, GROUP - 1)),
            dma((ITERS + 1, GROUP - 1)),
            dma((ITERS + 1, GROUP - 1)),
            dma((ITERS + 1, GROUP - 1)),
        ],
        compiler_params=pltpu.CompilerParams(collective_id=0, has_side_effects=True),
        name="first",
    )(
        pieces.reshape(piece_count, count, rows, lanes),
        giant_pieces.reshape(bands, GROUP, strip, side),
        giant_footprint[0],
        jnp.broadcast_to(giant_spectra.reshape(table, 1), (table, lanes)),
        psf_matrix,
    )

    summed = pl.pallas_call(
        segment_kernel,
        out_shape=jax.ShapeDtypeStruct((blend_count, rows, lanes), BF16),
        in_specs=[SMEM, VMEM],
        out_specs=VMEM,
        scratch_shapes=[pltpu.VMEM((blend_count, rows, lanes), F32)],
        name="segment",
    )(homes, recv.reshape(count * piece_count, rows, lanes))

    image = pl.pallas_call(
        functools.partial(owner_kernel, count, owned),
        out_shape=jax.ShapeDtypeStruct((owned, count, rows, lanes), BF16),
        in_specs=[VMEM],
        out_specs=VMEM,
        scratch_shapes=[dma, dma((count - 1,)), dma((count - 1,))],
        compiler_params=pltpu.CompilerParams(collective_id=1, has_side_effects=True),
        name="owner",
    )(summed)

    active = (jnp.arange(sources, dtype=jnp.int32)[None, :] < source_count[:, None]).astype(F32)
    active_rows = jnp.broadcast_to(
        jnp.repeat(active, bands, axis=1)[:, :, None], (owned, table, lanes)
    )
    spectra_rows = jnp.broadcast_to(spectra.reshape(owned, table, 1), (owned, table, lanes))
    final_morph, sed_rows, model = pl.pallas_call(
        functools.partial(blend_kernel, bands, sources),
        grid=(owned,),
        out_shape=(
            jax.ShapeDtypeStruct((owned, sources, side, side), BF16),
            jax.ShapeDtypeStruct((owned, table, lanes), F32),
            jax.ShapeDtypeStruct((owned, bands, side, side), BF16),
        ),
        in_specs=[
            pl.BlockSpec((1, bands, side, side), lambda n: (n, 0, 0, 0)),
            pl.BlockSpec((1, side, side), lambda n: (n, 0, 0)),
            pl.BlockSpec((1, table, lanes), lambda n: (n, 0, 0)),
            pl.BlockSpec((1, table, lanes), lambda n: (n, 0, 0)),
            pl.BlockSpec((bands, side, side), lambda n: (0, 0, 0)),
        ],
        out_specs=(
            pl.BlockSpec((1, sources, side, side), lambda n: (n, 0, 0, 0)),
            pl.BlockSpec((1, table, lanes), lambda n: (n, 0, 0)),
            pl.BlockSpec((1, bands, side, side), lambda n: (n, 0, 0, 0)),
        ),
        scratch_shapes=[
            pltpu.VMEM((sources, side, side), F32),
            pltpu.VMEM((table, lanes), F32),
            pltpu.VMEM((bands, side, side), F32),
            pltpu.VMEM((table, lanes), F32),
            pltpu.VMEM((table, lanes), F32),
        ],
        name="blend",
    )(
        image.reshape(owned, bands, side, side),
        footprint,
        spectra_rows,
        active_rows,
        psf_matrix,
    )
    final_sed = sed_rows[:, :, 0].reshape(owned, sources, bands).astype(BF16)

    piece_model = pl.pallas_call(
        functools.partial(return_kernel, count, owned, piece_count),
        out_shape=jax.ShapeDtypeStruct((piece_count, count, rows, lanes), BF16),
        in_specs=[SMEM, VMEM],
        out_specs=VMEM,
        scratch_shapes=[
            pltpu.VMEM((blend_count, rows, lanes), BF16),
            pltpu.VMEM((count, piece_count, rows, lanes), BF16),
            dma((2,)),
            dma((count - 1,)),
            dma((count - 1,)),
            dma((count - 1,)),
            dma((count - 1,)),
        ],
        compiler_params=pltpu.CompilerParams(collective_id=2, has_side_effects=True),
        name="back",
    )(homes, model.reshape(owned, count, rows, lanes))

    tile_model = pl.pallas_call(
        functools.partial(place_kernel, side),
        grid=(bands,),
        out_shape=jax.ShapeDtypeStruct((bands, TILE, TILE), F32),
        in_specs=[SMEM, pl.BlockSpec((piece_count, 1, side, side), lambda b: (0, b, 0, 0))],
        out_specs=pl.BlockSpec((1, TILE, TILE), lambda b: (b, 0, 0)),
        scratch_shapes=[
            pltpu.VMEM((piece_count, TILE, side), BF16),
            pltpu.VMEM((piece_count, side, TILE), BF16),
        ],
        name="place",
    )(corners, piece_model.reshape(piece_count, bands, side, side))
    return (final_morph, final_sed, tile_model[None], giant_morph[None])


def solution(mesh):
    in_specs = (
        P(("groups", "tiles"), None, None, None),
        P(("groups", "tiles")),
        P(("groups", "tiles"), None),
        P("groups"),
        P(("groups", "tiles")),
        P(("groups", "tiles"), None, None),
        P(("groups", "tiles"), None, None),
        P(("groups", "tiles"), None, None, None),
        P(("groups", "tiles"), None, None),
        P(("groups", "tiles"), None, None),
        P(),
    )
    out_specs = (
        P(("groups", "tiles"), None, None, None),
        P(("groups", "tiles"), None, None),
        P(("groups", "tiles"), None, None, None),
        P(("groups", "tiles"), None, None, None),
    )
    return jax.shard_map(
        on_device, mesh=mesh, in_specs=in_specs, out_specs=out_specs, check_vma=False
    )
```

```python
import functools

import jax
import jax.numpy as jnp
from jax import lax
from jax.experimental import pallas as pl
from jax.experimental.pallas import tpu as pltpu
from jax.sharding import PartitionSpec as P

TILE = 256
ITERS = 3
GROUP = 8
MESH = pl.DeviceIdType.MESH
F32 = jnp.float32
BF16 = jnp.bfloat16

step_size = 0.1

VMEM = pl.BlockSpec(memory_space=pltpu.VMEM)
SMEM = pl.BlockSpec(memory_space=pltpu.SMEM)
ANY = pl.BlockSpec(memory_space=pl.ANY)


def matmul(a, b):
    return jnp.dot(a, b, preferred_element_type=F32)


def matmul_t(a, b):
    return lax.dot_general(a, b, (((1,), (1,)), ((), ())), preferred_element_type=F32)


def t_matmul(a, b):
    return lax.dot_general(a, b, (((0,), (0,)), ((), ())), preferred_element_type=F32)


def barrier_all(me, count):
    barrier = pltpu.get_barrier_semaphore()
    for k in range(1, count):
        pl.semaphore_signal(
            barrier, inc=1, device_id={"tiles": lax.rem(me + k, count)}, device_id_type=MESH
        )
    pl.semaphore_wait(barrier, count - 1)


def remote(src, dst, send_sem, recv_sem, peer):
    return pltpu.make_async_remote_copy(
        src_ref=src,
        dst_ref=dst,
        send_sem=send_sem,
        recv_sem=recv_sem,
        device_id={"tiles": peer},
        device_id_type=MESH,
    )


def mix_band(sed_ref, morph_ref, b, bands, sources):
    total = sed_ref[b : b + 1, :] * morph_ref[0]
    for k in range(1, sources):
        row = k * bands + b
        total = total + sed_ref[row : row + 1, :] * morph_ref[k]
    return total.astype(BF16)


def blur_band(mix, kernel):
    return matmul_t(matmul(kernel, mix).astype(BF16), kernel)


def adjoint_band(resid, kernel):
    return matmul(t_matmul(kernel, resid).astype(BF16), kernel)


def update(sed_ref, morph_ref, grad_ref, part_ref, energy_ref, act_rows, bands, sources):
    for k in range(sources):
        morph = morph_ref[k]
        energy = jnp.sum(morph * morph, axis=0, keepdims=True)
        push = None
        for b in range(bands):
            row = k * bands + b
            grad = grad_ref[b]
            part_ref[row : row + 1, :] = jnp.sum(morph * grad, axis=0, keepdims=True)
            energy_ref[row : row + 1, :] = energy
            term = sed_ref[row : row + 1, :] * grad
            push = term if push is None else push + term
        fresh = jnp.maximum(morph + step_size * push, 0.0)
        if act_rows is not None:
            fresh = fresh * act_rows[k * bands : k * bands + 1, :]
        morph_ref[k] = fresh
    inner = jnp.sum(part_ref[...], axis=1, keepdims=True)
    energy = jnp.sum(energy_ref[...], axis=1, keepdims=True)
    sed = jnp.maximum(sed_ref[...] + inner / (energy + 1.0), 0.0)
    if act_rows is not None:
        sed = sed * act_rows[...]
    sed_ref[...] = sed


def first_kernel(
    count,
    bands,
    sources,
    pieces_ref,
    home_ref,
    giant_ref,
    labels_ref,
    spectra_ref,
    psf_ref,
    recv_ref,
    morph_ref,
    homes_ref,
    scatter_buf,
    base_buf,
    resid_buf,
    blurred,
    image_part,
    sed_ref,
    grad_ref,
    part_ref,
    energy_ref,
    own_sem,
    send_sem,
    recv_sem,
    rs_send,
    rs_recv,
    ag_send,
    ag_recv,
    home_send,
    home_recv,
):
    me = lax.axis_index("tiles")
    rank = lax.rem(me, GROUP)
    base = me - rank
    barrier = pltpu.get_barrier_semaphore()
    for k in range(1, GROUP):
        pl.semaphore_signal(
            barrier,
            inc=1,
            device_id={"tiles": base + lax.rem(rank + k, GROUP)},
            device_id_type=MESH,
        )
    pl.semaphore_wait(barrier, GROUP - 1)

    def scatter_copies(slot, src):
        copies = []
        for k in range(1, GROUP):
            other = lax.rem(rank + k, GROUP)
            copies.append(
                remote(
                    src.at[:, other],
                    scatter_buf.at[slot, rank],
                    rs_send.at[slot, k - 1],
                    rs_recv.at[slot, k - 1],
                    base + other,
                )
            )
        return copies

    def gather_copies(slot, ref):
        copies = []
        for k in range(1, GROUP):
            other = lax.rem(rank + k, GROUP)
            copies.append(
                remote(
                    ref.at[rank],
                    ref.at[rank],
                    ag_send.at[slot, k - 1],
                    ag_recv.at[slot, k - 1],
                    base + other,
                )
            )
        return copies

    def others_sum(slot, own):
        total = own.astype(F32)
        for k in range(1, GROUP):
            source = lax.rem(rank + GROUP - k, GROUP)
            total = total + scatter_buf[slot, source].astype(F32)
        return total

    opening = scatter_copies(ITERS, giant_ref)
    for copy in opening:
        copy.start()
    homes_ref[rank] = home_ref[...]
    exchange = []
    for k in range(1, GROUP):
        other = lax.rem(rank + k, GROUP)
        exchange.append(
            remote(
                home_ref,
                homes_ref.at[rank],
                home_send.at[k - 1],
                home_recv.at[k - 1],
                base + other,
            )
        )
    for k in range(1, GROUP):
        other = lax.rem(rank + k, GROUP)
        exchange.append(
            remote(
                pieces_ref.at[:, other],
                recv_ref.at[rank],
                send_sem.at[k - 1],
                recv_sem.at[k - 1],
                base + other,
            )
        )
    for copy in exchange:
        copy.start()
    own = pltpu.make_async_copy(pieces_ref.at[:, rank], recv_ref.at[rank], own_sem)
    own.start()

    for copy in opening:
        copy.wait_recv()
    image = others_sum(ITERS, giant_ref[:, rank])
    image_part[...] = image
    mean = image[0]
    for b in range(1, bands):
        mean = mean + image[b]
    base_buf[rank] = jnp.maximum(mean / bands, 0.0)
    spread = gather_copies(ITERS, base_buf)
    for copy in spread:
        copy.start()
    sed_ref[...] = spectra_ref[...]
    for copy in spread:
        copy.wait()
    for copy in opening:
        copy.wait_send()
    side = labels_ref.shape[0]
    base_map = base_buf[...].reshape(side, side)
    for k in range(sources):
        morph_ref[k] = jnp.where(labels_ref[...] == k + 1, base_map, 0.0)

    def iteration(it, carry):
        for b in range(bands):
            mix = mix_band(sed_ref, morph_ref, b, bands, sources)
            blurred[it, b] = (
                blur_band(mix, psf_ref[b]).astype(BF16).reshape(GROUP, side // GROUP, side)
            )
        sends = scatter_copies(it, blurred.at[it])
        for copy in sends:
            copy.start()
        for copy in sends:
            copy.wait()
        model = others_sum(it, blurred[it, :, rank])
        resid_buf[it, rank] = (image_part[...] - model).astype(BF16)
        shares = gather_copies(it, resid_buf.at[it])
        for copy in shares:
            copy.start()
        for copy in shares:
            copy.wait()
        for b in range(bands):
            resid = resid_buf[it, :, b].reshape(side, side)
            grad_ref[b] = adjoint_band(resid, psf_ref[b])
        update(sed_ref, morph_ref, grad_ref, part_ref, energy_ref, None, bands, sources)
        return carry

    lax.fori_loop(0, ITERS, iteration, 0)
    own.wait()
    for copy in exchange:
        copy.wait()


def segment_kernel(homes_ref, recv_ref, out_ref, total):
    total[...] = jnp.zeros_like(total)

    def add(index, carry):
        home = homes_ref[index]
        total[home] = total[home] + recv_ref[index].astype(F32)
        return carry

    lax.fori_loop(0, recv_ref.shape[0], add, 0, unroll=4)
    out_ref[...] = total[...].astype(BF16)


def core_kernel(
    count,
    bands,
    sources,
    owned,
    piece_count,
    homes_ref,
    summed_ref,
    labels_ref,
    spectra_ref,
    active_ref,
    psf_ref,
    out_morph,
    out_sed,
    out_ref,
    arrived,
    image_ref,
    morph_ref,
    sed_ref,
    grad_ref,
    part_ref,
    energy_ref,
    model_ref,
    held,
    picked,
    own_sems,
    in_send,
    in_recv,
    back_send,
    back_recv,
    last_send,
    last_recv,
):
    me = lax.axis_index("tiles")
    rank = lax.rem(me, GROUP)
    base = me - rank
    mine = me // GROUP
    groups = count // GROUP
    side = labels_ref.shape[1]
    barrier_all(me, count)

    def incoming(n, k):
        peer = lax.rem(me + k, count)
        return remote(
            summed_ref.at[peer * owned + n],
            arrived.at[n, mine, rank],
            in_send.at[n, k - 1],
            in_recv.at[n, k - 1],
            peer,
        )

    def outgoing(n, k):
        peer = lax.rem(me + k, count)
        return remote(
            model_ref.at[n, lax.rem(peer, GROUP)],
            held.at[me * owned + n],
            back_send.at[n, k - 1],
            back_recv.at[n, k - 1],
            peer,
        )

    def launch(n, carry):
        for k in range(1, count):
            incoming(n, k).start()
        return carry

    lax.fori_loop(0, owned, launch, 0)

    def blend(n, carry):
        arrived[n, mine, rank] = summed_ref[me * owned + n]
        for k in range(1, count):
            incoming(n, k).wait_recv()
        total = arrived[n, 0].astype(F32)
        for g in range(1, groups):
            total = total + arrived[n, g].astype(F32)
        image_ref[...] = total.reshape(bands, side, side)
        act = active_ref.at[n]
        sed_ref[...] = spectra_ref[n] * active_ref[n]
        mean = image_ref[0]
        for b in range(1, bands):
            mean = mean + image_ref[b]
        base_map = jnp.maximum(mean / bands, 0.0)
        for k in range(sources):
            morph_ref[k] = (
                jnp.where(labels_ref[n] == k + 1, base_map, 0.0)
                * act[k * bands : k * bands + 1, :]
            )

        def iteration(it, carry):
            for b in range(bands):
                kernel = psf_ref[b]
                mix = mix_band(sed_ref, morph_ref, b, bands, sources)
                resid = (image_ref[b] - blur_band(mix, kernel)).astype(BF16)
                grad_ref[b] = adjoint_band(resid, kernel)
            update(sed_ref, morph_ref, grad_ref, part_ref, energy_ref, act, bands, sources)
            return carry

        lax.fori_loop(0, ITERS, iteration, 0)
        out_morph[n] = morph_ref[...].astype(BF16)
        morph_ref[...] = morph_ref[...].astype(BF16).astype(F32)
        sed_ref[...] = sed_ref[...].astype(BF16).astype(F32)
        out_sed[n] = sed_ref[...]
        for b in range(bands):
            mix = mix_band(sed_ref, morph_ref, b, bands, sources)
            grad_ref[b] = blur_band(mix, psf_ref[b])
        model_ref[n] = grad_ref[...].reshape(model_ref.shape[1:]).astype(BF16)
        held[me * owned + n] = model_ref[n, rank]
        for k in range(1, count):
            outgoing(n, k).start()
        return carry

    lax.fori_loop(0, owned, blend, 0)

    def settle(n, carry):
        for k in range(1, count):
            incoming(n, k).wait_send()
        for k in range(1, count):
            outgoing(n, k).wait()
        return carry

    lax.fori_loop(0, owned, settle, 0)

    def pick(target):
        def one(index, carry):
            picked[target, index] = held[homes_ref[target * piece_count + index]]
            return carry

        lax.fori_loop(0, piece_count, one, 0, unroll=4)

    answers = []
    for k in range(1, GROUP):
        other = lax.rem(rank + k, GROUP)
        pick(other)
        copy = remote(
            picked.at[other],
            out_ref.at[:, rank],
            last_send.at[k - 1],
            last_recv.at[k - 1],
            base + other,
        )
        copy.start()
        answers.append(copy)
    pick(rank)
    last = pltpu.make_async_copy(picked.at[rank], out_ref.at[:, rank], own_sems)
    last.start()
    last.wait()
    for copy in answers:
        copy.wait()


def place_kernel(side, corners_ref, model_ref, out_ref, row_hot, col_hot):
    piece_count = model_ref.shape[0]

    @pl.when(pl.program_id(0) == 0)
    def _():
        rows = lax.broadcasted_iota(jnp.int32, (TILE, side), 0)
        inner = lax.broadcasted_iota(jnp.int32, (TILE, side), 1)
        inner_c = lax.broadcasted_iota(jnp.int32, (side, TILE), 0)
        cols = lax.broadcasted_iota(jnp.int32, (side, TILE), 1)

        def build(index, carry):
            row_hot[index] = jnp.where(rows == inner + corners_ref[index, 0], 1.0, 0.0).astype(BF16)
            col_hot[index] = jnp.where(cols == inner_c + corners_ref[index, 1], 1.0, 0.0).astype(
                BF16
            )
            return carry

        lax.fori_loop(0, piece_count, build, 0)

    total = jnp.zeros((TILE, TILE), F32)
    for index in range(piece_count):
        wide = matmul(model_ref[index, 0], col_hot[index]).astype(BF16)
        total = total + matmul(row_hot[index], wide)
    out_ref[0] = total


def on_device(
    pieces,
    piece_blend,
    corners,
    blend_home,
    source_count,
    footprint,
    spectra,
    giant_pieces,
    giant_footprint,
    giant_spectra,
    psf_matrix,
):
    count = lax.axis_size("tiles")
    piece_count, bands, side, _ = pieces.shape
    owned = footprint.shape[0]
    blend_count = blend_home.shape[0]
    sources = spectra.shape[1]
    rows = bands * side // GROUP
    groups = count // GROUP
    lanes = side
    table = sources * bands
    lookup = piece_blend[:, None] == jnp.arange(blend_count, dtype=jnp.int32)[None, :]
    piece_home = jnp.sum(jnp.where(lookup, blend_home[None, :], 0), axis=1)
    home_rows = jnp.broadcast_to(jnp.pad(piece_home, (0, side - piece_count)), (8, side))

    dma = pltpu.SemaphoreType.DMA
    strip = side // GROUP
    recv, giant_morph, every_home = pl.pallas_call(
        functools.partial(first_kernel, count, bands, sources),
        out_shape=(
            jax.ShapeDtypeStruct((GROUP, piece_count, rows, lanes), BF16),
            jax.ShapeDtypeStruct((sources, side, side), F32),
            jax.ShapeDtypeStruct((GROUP, 8, side), jnp.int32),
        ),
        in_specs=[ANY, VMEM, VMEM, VMEM, VMEM, VMEM],
        out_specs=(ANY, VMEM, VMEM),
        scratch_shapes=[
            pltpu.VMEM((ITERS + 1, GROUP, bands, strip, side), BF16),
            pltpu.VMEM((GROUP, strip, side), F32),
            pltpu.VMEM((ITERS, GROUP, bands, strip, side), BF16),
            pltpu.VMEM((ITERS, bands, GROUP, strip, side), BF16),
            pltpu.VMEM((bands, strip, side), F32),
            pltpu.VMEM((table, lanes), F32),
            pltpu.VMEM((bands, side, side), F32),
            pltpu.VMEM((table, lanes), F32),
            pltpu.VMEM((table, lanes), F32),
            dma,
            dma((GROUP - 1,)),
            dma((GROUP - 1,)),
            dma((ITERS + 1, GROUP - 1)),
            dma((ITERS + 1, GROUP - 1)),
            dma((ITERS + 1, GROUP - 1)),
            dma((ITERS + 1, GROUP - 1)),
            dma((GROUP - 1,)),
            dma((GROUP - 1,)),
        ],
        compiler_params=pltpu.CompilerParams(collective_id=0, has_side_effects=True),
        name="first",
    )(
        pieces.reshape(piece_count, GROUP, rows, lanes),
        home_rows,
        giant_pieces.reshape(bands, GROUP, strip, side),
        giant_footprint[0],
        jnp.broadcast_to(giant_spectra.reshape(table, 1), (table, lanes)),
        psf_matrix,
    )

    homes = every_home[:, 0, :piece_count].reshape(-1)
    summed = pl.pallas_call(
        segment_kernel,
        out_shape=jax.ShapeDtypeStruct((blend_count, rows, lanes), BF16),
        in_specs=[SMEM, VMEM],
        out_specs=VMEM,
        scratch_shapes=[pltpu.VMEM((blend_count, rows, lanes), F32)],
        name="segment",
    )(homes, recv.reshape(GROUP * piece_count, rows, lanes))

    active = (jnp.arange(sources, dtype=jnp.int32)[None, :] < source_count[:, None]).astype(F32)
    active_rows = jnp.broadcast_to(
        jnp.repeat(active, bands, axis=1)[:, :, None], (owned, table, lanes)
    )
    spectra_rows = jnp.broadcast_to(spectra.reshape(owned, table, 1), (owned, table, lanes))
    chunk = (GROUP, rows, lanes)
    final_morph, sed_rows, piece_model = pl.pallas_call(
        functools.partial(core_kernel, count, bands, sources, owned, piece_count),
        out_shape=(
            jax.ShapeDtypeStruct((owned, sources, side, side), BF16),
            jax.ShapeDtypeStruct((owned, table, lanes), F32),
            jax.ShapeDtypeStruct((piece_count, GROUP, rows, lanes), BF16),
        ),
        in_specs=[SMEM, VMEM, VMEM, VMEM, VMEM, VMEM],
        out_specs=(VMEM, VMEM, VMEM),
        scratch_shapes=[
            pltpu.VMEM((owned, groups) + chunk, BF16),
            pltpu.VMEM((bands, side, side), F32),
            pltpu.VMEM((sources, side, side), F32),
            pltpu.VMEM((table, lanes), F32),
            pltpu.VMEM((bands, side, side), F32),
            pltpu.VMEM((table, lanes), F32),
            pltpu.VMEM((table, lanes), F32),
            pltpu.VMEM((owned,) + chunk, BF16),
            pltpu.VMEM((blend_count, rows, lanes), BF16),
            pltpu.VMEM((GROUP, piece_count, rows, lanes), BF16),
            dma,
            dma((owned, count - 1)),
            dma((owned, count - 1)),
            dma((owned, count - 1)),
            dma((owned, count - 1)),
            dma((GROUP - 1,)),
            dma((GROUP - 1,)),
        ],
        compiler_params=pltpu.CompilerParams(collective_id=1, has_side_effects=True),
        name="core",
    )(homes, summed, footprint, spectra_rows, active_rows, psf_matrix)
    final_sed = sed_rows[:, :, 0].reshape(owned, sources, bands).astype(BF16)

    tile_model = pl.pallas_call(
        functools.partial(place_kernel, side),
        grid=(bands,),
        out_shape=jax.ShapeDtypeStruct((bands, TILE, TILE), F32),
        in_specs=[SMEM, pl.BlockSpec((piece_count, 1, side, side), lambda b: (0, b, 0, 0))],
        out_specs=pl.BlockSpec((1, TILE, TILE), lambda b: (b, 0, 0)),
        scratch_shapes=[
            pltpu.VMEM((piece_count, TILE, side), BF16),
            pltpu.VMEM((piece_count, side, TILE), BF16),
        ],
        name="place",
    )(corners, piece_model.reshape(piece_count, bands, side, side))
    return (final_morph, final_sed, tile_model[None], giant_morph[None])


def solution(mesh):
    in_specs = (
        P(("groups", "tiles"), None, None, None),
        P(("groups", "tiles")),
        P(("groups", "tiles"), None),
        P("groups"),
        P(("groups", "tiles")),
        P(("groups", "tiles"), None, None),
        P(("groups", "tiles"), None, None),
        P(("groups", "tiles"), None, None, None),
        P(("groups", "tiles"), None, None),
        P(("groups", "tiles"), None, None),
        P(),
    )
    out_specs = (
        P(("groups", "tiles"), None, None, None),
        P(("groups", "tiles"), None, None),
        P(("groups", "tiles"), None, None, None),
        P(("groups", "tiles"), None, None, None),
    )
    return jax.shard_map(
        on_device, mesh=mesh, in_specs=in_specs, out_specs=out_specs, check_vma=False
    )
```

```python
import functools

import jax
import jax.numpy as jnp
from jax import lax
from jax.experimental import pallas as pl
from jax.experimental.pallas import tpu as pltpu
from jax.sharding import PartitionSpec as P

TILE = 256
ITERS = 3
GROUP = 8
MESH = pl.DeviceIdType.MESH
F32 = jnp.float32
BF16 = jnp.bfloat16

step_size = 0.1

VMEM = pl.BlockSpec(memory_space=pltpu.VMEM)
SMEM = pl.BlockSpec(memory_space=pltpu.SMEM)
ANY = pl.BlockSpec(memory_space=pl.ANY)


def matmul(a, b):
    return jnp.dot(a, b, preferred_element_type=F32)


def matmul_t(a, b):
    return lax.dot_general(a, b, (((1,), (1,)), ((), ())), preferred_element_type=F32)


def t_matmul(a, b):
    return lax.dot_general(a, b, (((0,), (0,)), ((), ())), preferred_element_type=F32)


def barrier_all(me, count):
    barrier = pltpu.get_barrier_semaphore()
    for k in range(1, count):
        pl.semaphore_signal(
            barrier, inc=1, device_id={"tiles": lax.rem(me + k, count)}, device_id_type=MESH
        )
    pl.semaphore_wait(barrier, count - 1)


def remote(src, dst, send_sem, recv_sem, peer):
    return pltpu.make_async_remote_copy(
        src_ref=src,
        dst_ref=dst,
        send_sem=send_sem,
        recv_sem=recv_sem,
        device_id={"tiles": peer},
        device_id_type=MESH,
    )


def mix_band(sed_ref, morph_ref, b, bands, sources):
    total = sed_ref[b : b + 1, :] * morph_ref[0]
    for k in range(1, sources):
        row = k * bands + b
        total = total + sed_ref[row : row + 1, :] * morph_ref[k]
    return total.astype(BF16)


def blur_band(mix, kernel):
    return matmul_t(matmul(kernel, mix).astype(BF16), kernel)


def adjoint_band(resid, kernel):
    return matmul(t_matmul(kernel, resid).astype(BF16), kernel)


def update(sed_ref, morph_ref, grad_ref, part_ref, energy_ref, act_rows, bands, sources):
    for k in range(sources):
        morph = morph_ref[k]
        energy = jnp.sum(morph * morph, axis=0, keepdims=True)
        push = None
        for b in range(bands):
            row = k * bands + b
            grad = grad_ref[b]
            part_ref[row : row + 1, :] = jnp.sum(morph * grad, axis=0, keepdims=True)
            energy_ref[row : row + 1, :] = energy
            term = sed_ref[row : row + 1, :] * grad
            push = term if push is None else push + term
        fresh = jnp.maximum(morph + step_size * push, 0.0)
        if act_rows is not None:
            fresh = fresh * act_rows[k * bands : k * bands + 1, :]
        morph_ref[k] = fresh
    inner = jnp.sum(part_ref[...], axis=1, keepdims=True)
    energy = jnp.sum(energy_ref[...], axis=1, keepdims=True)
    sed = jnp.maximum(sed_ref[...] + inner / (energy + 1.0), 0.0)
    if act_rows is not None:
        sed = sed * act_rows[...]
    sed_ref[...] = sed


def first_kernel(
    count,
    bands,
    sources,
    pieces_ref,
    home_ref,
    giant_ref,
    labels_ref,
    spectra_ref,
    psf_ref,
    recv_ref,
    morph_ref,
    homes_ref,
    scatter_buf,
    base_buf,
    resid_buf,
    blurred,
    image_part,
    sed_ref,
    grad_ref,
    part_ref,
    energy_ref,
    own_sem,
    send_sem,
    recv_sem,
    rs_send,
    rs_recv,
    ag_send,
    ag_recv,
    home_send,
    home_recv,
):
    me = lax.axis_index("tiles")
    rank = lax.rem(me, GROUP)
    base = me - rank
    barrier = pltpu.get_barrier_semaphore()
    for k in range(1, GROUP):
        pl.semaphore_signal(
            barrier,
            inc=1,
            device_id={"tiles": base + lax.rem(rank + k, GROUP)},
            device_id_type=MESH,
        )
    pl.semaphore_wait(barrier, GROUP - 1)

    def scatter_copies(slot, src):
        copies = []
        for k in range(1, GROUP):
            other = lax.rem(rank + k, GROUP)
            copies.append(
                remote(
                    src.at[:, other],
                    scatter_buf.at[slot, rank],
                    rs_send.at[slot, k - 1],
                    rs_recv.at[slot, k - 1],
                    base + other,
                )
            )
        return copies

    def gather_copies(slot, ref):
        copies = []
        for k in range(1, GROUP):
            other = lax.rem(rank + k, GROUP)
            copies.append(
                remote(
                    ref.at[rank],
                    ref.at[rank],
                    ag_send.at[slot, k - 1],
                    ag_recv.at[slot, k - 1],
                    base + other,
                )
            )
        return copies

    def others_sum(slot, own):
        total = own.astype(F32)
        for k in range(1, GROUP):
            source = lax.rem(rank + GROUP - k, GROUP)
            total = total + scatter_buf[slot, source].astype(F32)
        return total

    opening = scatter_copies(ITERS, giant_ref)
    for copy in opening:
        copy.start()
    homes_ref[rank] = home_ref[...]
    exchange = []
    for k in range(1, GROUP):
        other = lax.rem(rank + k, GROUP)
        exchange.append(
            remote(
                home_ref,
                homes_ref.at[rank],
                home_send.at[k - 1],
                home_recv.at[k - 1],
                base + other,
            )
        )
    def piece_copy(k):
        other = lax.rem(rank + k, GROUP)
        return remote(
            pieces_ref.at[:, other],
            recv_ref.at[rank],
            send_sem.at[k - 1],
            recv_sem.at[k - 1],
            base + other,
        )

    for copy in exchange:
        copy.start()
    late = (GROUP - 1) // ITERS
    early = GROUP - 1 - late * ITERS
    for k in range(1, early + 1):
        piece_copy(k).start()
    own = pltpu.make_async_copy(pieces_ref.at[:, rank], recv_ref.at[rank], own_sem)
    own.start()

    for copy in opening:
        copy.wait_recv()
    image = others_sum(ITERS, giant_ref[:, rank])
    image_part[...] = image
    mean = image[0]
    for b in range(1, bands):
        mean = mean + image[b]
    base_buf[rank] = jnp.maximum(mean / bands, 0.0)
    spread = gather_copies(ITERS, base_buf)
    for copy in spread:
        copy.start()
    sed_ref[...] = spectra_ref[...]
    for copy in spread:
        copy.wait()
    for copy in opening:
        copy.wait_send()
    side = labels_ref.shape[0]
    base_map = base_buf[...].reshape(side, side)
    for k in range(sources):
        morph_ref[k] = jnp.where(labels_ref[...] == k + 1, base_map, 0.0)

    def iteration(it, carry):
        for offset in range(late):
            piece_copy(early + 1 + it * late + offset).start()
        for b in range(bands):
            mix = mix_band(sed_ref, morph_ref, b, bands, sources)
            blurred[it, b] = (
                blur_band(mix, psf_ref[b]).astype(BF16).reshape(GROUP, side // GROUP, side)
            )
        sends = scatter_copies(it, blurred.at[it])
        for copy in sends:
            copy.start()
        for copy in sends:
            copy.wait()
        model = others_sum(it, blurred[it, :, rank])
        resid_buf[it, rank] = (image_part[...] - model).astype(BF16)
        shares = gather_copies(it, resid_buf.at[it])
        for copy in shares:
            copy.start()
        for copy in shares:
            copy.wait()
        for b in range(bands):
            resid = resid_buf[it, :, b].reshape(side, side)
            grad_ref[b] = adjoint_band(resid, psf_ref[b])
        update(sed_ref, morph_ref, grad_ref, part_ref, energy_ref, None, bands, sources)
        return carry

    lax.fori_loop(0, ITERS, iteration, 0)
    own.wait()
    for copy in exchange:
        copy.wait()
    for k in range(1, GROUP):
        piece_copy(k).wait()


def segment_kernel(homes_ref, recv_ref, out_ref, total):
    total[...] = jnp.zeros_like(total)

    def add(index, carry):
        home = homes_ref[index]
        total[home] = total[home] + recv_ref[index].astype(F32)
        return carry

    lax.fori_loop(0, recv_ref.shape[0], add, 0, unroll=4)
    out_ref[...] = total[...].astype(BF16)


def core_kernel(
    count,
    bands,
    sources,
    owned,
    piece_count,
    homes_ref,
    summed_ref,
    labels_ref,
    spectra_ref,
    active_ref,
    psf_ref,
    out_morph,
    out_sed,
    out_ref,
    arrived,
    image_ref,
    morph_ref,
    sed_ref,
    grad_ref,
    part_ref,
    energy_ref,
    model_ref,
    held,
    picked,
    own_sems,
    in_send,
    in_recv,
    back_send,
    back_recv,
    last_send,
    last_recv,
):
    me = lax.axis_index("tiles")
    rank = lax.rem(me, GROUP)
    base = me - rank
    mine = me // GROUP
    groups = count // GROUP
    side = labels_ref.shape[1]
    barrier_all(me, count)

    def incoming(n, k):
        peer = lax.rem(me + k, count)
        return remote(
            summed_ref.at[peer * owned + n],
            arrived.at[n, mine, rank],
            in_send.at[n, k - 1],
            in_recv.at[n, k - 1],
            peer,
        )

    def outgoing(n, k):
        peer = lax.rem(me + k, count)
        return remote(
            model_ref.at[n, lax.rem(peer, GROUP)],
            held.at[me * owned + n],
            back_send.at[n, k - 1],
            back_recv.at[n, k - 1],
            peer,
        )

    def launch(n, carry):
        for k in range(1, count):
            incoming(n, k).start()
        return carry

    lax.fori_loop(0, owned, launch, 0)

    def blend(n, carry):
        arrived[n, mine, rank] = summed_ref[me * owned + n]
        for k in range(1, count):
            incoming(n, k).wait_recv()
        total = arrived[n, 0].astype(F32)
        for g in range(1, groups):
            total = total + arrived[n, g].astype(F32)
        image_ref[...] = total.reshape(bands, side, side)
        act = active_ref.at[n]
        sed_ref[...] = spectra_ref[n] * active_ref[n]
        mean = image_ref[0]
        for b in range(1, bands):
            mean = mean + image_ref[b]
        base_map = jnp.maximum(mean / bands, 0.0)
        for k in range(sources):
            morph_ref[k] = (
                jnp.where(labels_ref[n] == k + 1, base_map, 0.0)
                * act[k * bands : k * bands + 1, :]
            )

        def iteration(it, carry):
            for b in range(bands):
                kernel = psf_ref[b]
                mix = mix_band(sed_ref, morph_ref, b, bands, sources)
                resid = (image_ref[b] - blur_band(mix, kernel)).astype(BF16)
                grad_ref[b] = adjoint_band(resid, kernel)
            update(sed_ref, morph_ref, grad_ref, part_ref, energy_ref, act, bands, sources)
            return carry

        lax.fori_loop(0, ITERS, iteration, 0)
        out_morph[n] = morph_ref[...].astype(BF16)
        morph_ref[...] = morph_ref[...].astype(BF16).astype(F32)
        sed_ref[...] = sed_ref[...].astype(BF16).astype(F32)
        out_sed[n] = sed_ref[...]
        for b in range(bands):
            mix = mix_band(sed_ref, morph_ref, b, bands, sources)
            grad_ref[b] = blur_band(mix, psf_ref[b])
        model_ref[n] = grad_ref[...].reshape(model_ref.shape[1:]).astype(BF16)
        held[me * owned + n] = model_ref[n, rank]
        for k in range(1, count):
            outgoing(n, k).start()
        return carry

    lax.fori_loop(0, owned, blend, 0)

    def settle(n, carry):
        for k in range(1, count):
            incoming(n, k).wait_send()
        for k in range(1, count):
            outgoing(n, k).wait()
        return carry

    lax.fori_loop(0, owned, settle, 0)

    def pick(target):
        def one(index, carry):
            picked[target, index] = held[homes_ref[target * piece_count + index]]
            return carry

        lax.fori_loop(0, piece_count, one, 0, unroll=4)

    answers = []
    for k in range(1, GROUP):
        other = lax.rem(rank + k, GROUP)
        pick(other)
        copy = remote(
            picked.at[other],
            out_ref.at[:, rank],
            last_send.at[k - 1],
            last_recv.at[k - 1],
            base + other,
        )
        copy.start()
        answers.append(copy)
    pick(rank)
    last = pltpu.make_async_copy(picked.at[rank], out_ref.at[:, rank], own_sems)
    last.start()
    last.wait()
    for copy in answers:
        copy.wait()


def place_kernel(side, corners_ref, model_ref, out_ref, row_hot, col_hot, wide):
    piece_count = model_ref.shape[0]

    @pl.when(pl.program_id(0) == 0)
    def _():
        rows = lax.broadcasted_iota(jnp.int32, (TILE, side), 0)
        inner = lax.broadcasted_iota(jnp.int32, (TILE, side), 1)
        inner_c = lax.broadcasted_iota(jnp.int32, (side, TILE), 0)
        cols = lax.broadcasted_iota(jnp.int32, (side, TILE), 1)

        for index in range(piece_count):
            row_hot[:, index * side : (index + 1) * side] = jnp.where(
                rows == inner + corners_ref[index, 0], 1.0, 0.0
            ).astype(BF16)
            col_hot[index] = jnp.where(cols == inner_c + corners_ref[index, 1], 1.0, 0.0).astype(
                BF16
            )

    for index in range(piece_count):
        wide[index * side : (index + 1) * side, :] = matmul(
            model_ref[index, 0], col_hot[index]
        ).astype(BF16)
    out_ref[0] = matmul(row_hot[...], wide[...])


def on_device(
    pieces,
    piece_blend,
    corners,
    blend_home,
    source_count,
    footprint,
    spectra,
    giant_pieces,
    giant_footprint,
    giant_spectra,
    psf_matrix,
):
    count = lax.axis_size("tiles")
    piece_count, bands, side, _ = pieces.shape
    owned = footprint.shape[0]
    blend_count = blend_home.shape[0]
    sources = spectra.shape[1]
    rows = bands * side // GROUP
    groups = count // GROUP
    lanes = side
    table = sources * bands
    lookup = piece_blend[:, None] == jnp.arange(blend_count, dtype=jnp.int32)[None, :]
    piece_home = jnp.sum(jnp.where(lookup, blend_home[None, :], 0), axis=1)
    home_rows = jnp.broadcast_to(jnp.pad(piece_home, (0, side - piece_count)), (8, side))

    dma = pltpu.SemaphoreType.DMA
    strip = side // GROUP
    recv, giant_morph, every_home = pl.pallas_call(
        functools.partial(first_kernel, count, bands, sources),
        out_shape=(
            jax.ShapeDtypeStruct((GROUP, piece_count, rows, lanes), BF16),
            jax.ShapeDtypeStruct((sources, side, side), F32),
            jax.ShapeDtypeStruct((GROUP, 8, side), jnp.int32),
        ),
        in_specs=[ANY, VMEM, VMEM, VMEM, VMEM, VMEM],
        out_specs=(ANY, VMEM, VMEM),
        scratch_shapes=[
            pltpu.VMEM((ITERS + 1, GROUP, bands, strip, side), BF16),
            pltpu.VMEM((GROUP, strip, side), F32),
            pltpu.VMEM((ITERS, GROUP, bands, strip, side), BF16),
            pltpu.VMEM((ITERS, bands, GROUP, strip, side), BF16),
            pltpu.VMEM((bands, strip, side), F32),
            pltpu.VMEM((table, lanes), F32),
            pltpu.VMEM((bands, side, side), F32),
            pltpu.VMEM((table, lanes), F32),
            pltpu.VMEM((table, lanes), F32),
            dma,
            dma((GROUP - 1,)),
            dma((GROUP - 1,)),
            dma((ITERS + 1, GROUP - 1)),
            dma((ITERS + 1, GROUP - 1)),
            dma((ITERS + 1, GROUP - 1)),
            dma((ITERS + 1, GROUP - 1)),
            dma((GROUP - 1,)),
            dma((GROUP - 1,)),
        ],
        compiler_params=pltpu.CompilerParams(collective_id=0, has_side_effects=True),
        name="first",
    )(
        pieces.reshape(piece_count, GROUP, rows, lanes),
        home_rows,
        giant_pieces.reshape(bands, GROUP, strip, side),
        giant_footprint[0],
        jnp.broadcast_to(giant_spectra.reshape(table, 1), (table, lanes)),
        psf_matrix,
    )

    homes = every_home[:, 0, :piece_count].reshape(-1)
    summed = pl.pallas_call(
        segment_kernel,
        out_shape=jax.ShapeDtypeStruct((blend_count, rows, lanes), BF16),
        in_specs=[SMEM, VMEM],
        out_specs=VMEM,
        scratch_shapes=[pltpu.VMEM((blend_count, rows, lanes), F32)],
        name="segment",
    )(homes, recv.reshape(GROUP * piece_count, rows, lanes))

    active = (jnp.arange(sources, dtype=jnp.int32)[None, :] < source_count[:, None]).astype(F32)
    active_rows = jnp.broadcast_to(
        jnp.repeat(active, bands, axis=1)[:, :, None], (owned, table, lanes)
    )
    spectra_rows = jnp.broadcast_to(spectra.reshape(owned, table, 1), (owned, table, lanes))
    chunk = (GROUP, rows, lanes)
    final_morph, sed_rows, piece_model = pl.pallas_call(
        functools.partial(core_kernel, count, bands, sources, owned, piece_count),
        out_shape=(
            jax.ShapeDtypeStruct((owned, sources, side, side), BF16),
            jax.ShapeDtypeStruct((owned, table, lanes), F32),
            jax.ShapeDtypeStruct((piece_count, GROUP, rows, lanes), BF16),
        ),
        in_specs=[SMEM, VMEM, VMEM, VMEM, VMEM, VMEM],
        out_specs=(VMEM, VMEM, VMEM),
        scratch_shapes=[
            pltpu.VMEM((owned, groups) + chunk, BF16),
            pltpu.VMEM((bands, side, side), F32),
            pltpu.VMEM((sources, side, side), F32),
            pltpu.VMEM((table, lanes), F32),
            pltpu.VMEM((bands, side, side), F32),
            pltpu.VMEM((table, lanes), F32),
            pltpu.VMEM((table, lanes), F32),
            pltpu.VMEM((owned,) + chunk, BF16),
            pltpu.VMEM((blend_count, rows, lanes), BF16),
            pltpu.VMEM((GROUP, piece_count, rows, lanes), BF16),
            dma,
            dma((owned, count - 1)),
            dma((owned, count - 1)),
            dma((owned, count - 1)),
            dma((owned, count - 1)),
            dma((GROUP - 1,)),
            dma((GROUP - 1,)),
        ],
        compiler_params=pltpu.CompilerParams(collective_id=1, has_side_effects=True),
        name="core",
    )(homes, summed, footprint, spectra_rows, active_rows, psf_matrix)
    final_sed = sed_rows[:, :, 0].reshape(owned, sources, bands).astype(BF16)

    tile_model = pl.pallas_call(
        functools.partial(place_kernel, side),
        grid=(bands,),
        out_shape=jax.ShapeDtypeStruct((bands, TILE, TILE), F32),
        in_specs=[SMEM, pl.BlockSpec((piece_count, 1, side, side), lambda b: (0, b, 0, 0))],
        out_specs=pl.BlockSpec((1, TILE, TILE), lambda b: (b, 0, 0)),
        scratch_shapes=[
            pltpu.VMEM((TILE, piece_count * side), BF16),
            pltpu.VMEM((piece_count, side, TILE), BF16),
            pltpu.VMEM((piece_count * side, TILE), BF16),
        ],
        name="place",
    )(corners, piece_model.reshape(piece_count, bands, side, side))
    return (final_morph, final_sed, tile_model[None], giant_morph[None])


def solution(mesh):
    in_specs = (
        P(("groups", "tiles"), None, None, None),
        P(("groups", "tiles")),
        P(("groups", "tiles"), None),
        P("groups"),
        P(("groups", "tiles")),
        P(("groups", "tiles"), None, None),
        P(("groups", "tiles"), None, None),
        P(("groups", "tiles"), None, None, None),
        P(("groups", "tiles"), None, None),
        P(("groups", "tiles"), None, None),
        P(),
    )
    out_specs = (
        P(("groups", "tiles"), None, None, None),
        P(("groups", "tiles"), None, None),
        P(("groups", "tiles"), None, None, None),
        P(("groups", "tiles"), None, None, None),
    )
    return jax.shard_map(
        on_device, mesh=mesh, in_specs=in_specs, out_specs=out_specs, check_vma=False
    )
```
